512 devices in a mesh: long: 32 (over y, z_hi, core), aq: 16 (over x, z_lo).
Axes of the slice: x: 4, y: 4, z: 16 (z_hi: 4, z_lo: 4; z = z_hi * 4 + z_lo), core: 2. Of those that a mesh axis runs over, the one named last changes fastest.
Arguments:
- column_seed: float32 [2, 64, 256, 2048], P(None, None, 'long', 'aq'), may hold values from -6 to 6
- head_seed: float32 [256, 2048], P(None, 'aq'), may hold values from -6 to 6
- texture: int32 [64, 256, 2048], P(None, 'long', 'aq'), may hold values from 0 to 11
- soil_table: float32 [3, 12], replicated, may hold values from 0.2 to 5
- active: int32 [256, 2048], P('long', 'aq'), may hold values 0 or 1
- conductance: float32 [256, 2048], P('long', 'aq'), may hold values from 0.2 to 2
- wells: int32 [256, 2048], P('long', 'aq'), may hold values from 0 to 32767
- transmissivity: float32 [256, 2048], P(None, 'aq'), may hold values from 0.1 to 1
- storage: float32 [256, 2048], P(None, 'aq'), may hold values from 0.01 to 0.1
Outputs:
- column_adjoint: float32 [2, 64, 256, 2048], P(None, None, 'long', 'aq')
- recharge_adjoint: float32 [256, 2048], P('long', 'aq')
- head_adjoint: float32 [256, 2048], P('long', 'aq')
The draws below stay inside these ranges and needn't reach their ends.
Inputs may be any that keep to these rules, and one draw needn't show every extreme that they name: `wells`: the well of column (x, y) lies in the aquifer cells of the same group of 128 second coordinates, with the index x' * 128 + y' mod 128.
All inputs are finite; a program needn't handle non-finite values. No bound on the sum of `active` on one device may be relied on, other than what follows from the above.
Results may differ from the reference program's by a relative error of at most 0.0001.
Values sent between devices are 32-bit elements; how exact they have to be, the bound alone decides.
A program may use at most 64 MiB of HBM per device.

```python
import math
import jax
import jax.numpy as jnp
from jax import lax

NZ = 64
NCLASS = 12
SWEEPS = 4
STEPS = 2
CY = 128
NX = 256
NY = 2048


def place_ends(drawn, rng, low, largest):
    longest = drawn.shape.index(max(drawn.shape))
    spots = []
    for shift in (0, 1):
        where = [jax.random.randint(jax.random.fold_in(rng, axis), (), 0, length) for axis, length in enumerate(drawn.shape)]
        where[longest] = (where[longest] + shift) % drawn.shape[longest]
        spots.append(tuple(where))
    return drawn.at[spots[0]].set(low).at[spots[1]].set(largest)


def shard_levels(key, shape, shards, low, high):
    def one(axis_at, parts):
        heights = jax.random.uniform(jax.random.fold_in(jax.random.fold_in(key, 6), axis_at), (parts,), jnp.float32, low / len(shards), high / len(shards))
        return jnp.repeat(jnp.exp(heights), shape[axis_at] // parts).reshape((-1,) + (1,) * (len(shape) - axis_at - 1))

    loudness = one(*shards[0])
    for cut in shards[1:]:
        loudness = loudness * one(*cut)
    return loudness


def noise(stream_key, extent, scale, most, split=(), dtype=jnp.bfloat16):
    entries = scale * jax.random.normal(stream_key, extent, jnp.float32)
    if split:
        entries = entries * shard_levels(stream_key, extent, split, -0.22, 0.18)
    return jnp.clip(entries, -most, most).astype(dtype)


def setup_inputs(seed: int = 0) -> dict:
    arg_keys = jax.random.split(jax.random.key(seed), 10)
    column_seed = noise(arg_keys[0], (2, NZ, NX, NY), 1.0, 6.0, ((2, 32), (3, 16)), jnp.float32)
    head_seed = noise(arg_keys[1], (NX, NY), 1.0, 6.0, ((1, 16),), jnp.float32)
    texture = place_ends(jax.random.randint(arg_keys[2], (NZ, NX, NY), 0, NCLASS), jax.random.fold_in(arg_keys[2], 1), 0, NCLASS - 1).astype(jnp.int32)
    soil_table = jnp.clip(jnp.exp(jax.random.uniform(arg_keys[3], (3, NCLASS), jnp.float32, math.log(0.2), math.log(5.0))), 0.2, 5.0)
    active = place_ends((jax.random.randint(arg_keys[4], (NX, NY), 0, 4) < 3).astype(jnp.int32), jax.random.fold_in(arg_keys[4], 1), 0, 1)
    conductance = jnp.clip(jnp.exp(math.log(2.0) - 2.3025851 * jax.random.uniform(arg_keys[5], (NX, NY), jnp.float32) ** shard_levels(arg_keys[5], (NX, NY), ((0, 32), (1, 16)), -0.2, 0.2)), 0.2, 2.0)
    wells = place_ends(jax.random.randint(arg_keys[6], (NX, NY), 0, NX * CY), jax.random.fold_in(arg_keys[6], 1), 0, (NX * CY) - 1).astype(jnp.int32)
    transmissivity = jnp.clip(jnp.exp(math.log(1.0) - 2.3025851 * jax.random.uniform(arg_keys[7], (NX, NY), jnp.float32) ** shard_levels(arg_keys[7], (NX, NY), ((1, 16),), -0.2, 0.2)), 0.1, 1.0)
    storage = jnp.clip(jnp.exp(math.log(0.1) - 2.3025851 * jax.random.uniform(arg_keys[8], (NX, NY), jnp.float32) ** shard_levels(arg_keys[8], (NX, NY), ((1, 16),), -0.2, 0.2)), 0.01, 0.1)
    return dict(column_seed=column_seed, head_seed=head_seed, texture=texture, soil_table=soil_table, active=active, conductance=conductance, wells=wells, transmissivity=transmissivity, storage=storage)


RELAX = 0.8


def lookup(texture, table_row):
    values = jnp.zeros(texture.shape, jnp.float32)
    for number in range(table_row.shape[0]):
        values = jnp.where(texture == number, table_row[number], values)
    return values


def column_solve(faces, forcing):
    layer_count = forcing.shape[0]
    ratios = []
    partials = []
    for layer_index in range(layer_count):
        diagonal = jnp.ones_like(forcing[0])
        if layer_index > 0:
            diagonal = diagonal + faces[layer_index - 1]
        if layer_index < layer_count - 1:
            diagonal = diagonal + faces[layer_index]
        if layer_index == 0:
            pivot_value = diagonal
            carried = forcing[0]
        else:
            pivot_value = diagonal - faces[layer_index - 1] * ratios[-1]
            carried = forcing[layer_index] + faces[layer_index - 1] * partials[-1]
        if layer_index < layer_count - 1:
            ratios.append(faces[layer_index] / pivot_value)
        partials.append(carried / pivot_value)
    solution = [partials[-1]]
    for layer_index in range(layer_count - 2, -1, -1):
        solution.append(partials[layer_index] + ratios[layer_index] * solution[-1])
    return jnp.stack(solution[::-1])


def face_arrays(padded_t, row_start, col_start, total_rows, total_cols):
    centre = padded_t[1:-1, 1:-1]
    row_ids = row_start + lax.broadcasted_iota(jnp.int32, centre.shape, 0)
    col_ids = col_start + lax.broadcasted_iota(jnp.int32, centre.shape, 1)
    east_face = jnp.where(row_ids + 1 < total_rows, 0.5 * (centre + padded_t[2:, 1:-1]), 0.0)
    west_face = jnp.where(row_ids >= 1, 0.5 * (centre + padded_t[:-2, 1:-1]), 0.0)
    north_face = jnp.where(col_ids + 1 < total_cols, 0.5 * (centre + padded_t[1:-1, 2:]), 0.0)
    south_face = jnp.where(col_ids >= 1, 0.5 * (centre + padded_t[1:-1, :-2]), 0.0)
    return east_face, west_face, north_face, south_face


def relax(forcing_head, face_set, storage, neighbours):
    east_face, west_face, north_face, south_face = face_set
    diagonal = storage + east_face + west_face + north_face + south_face
    estimate = jnp.zeros_like(forcing_head)
    for sweep_number in range(SWEEPS):
        padded = neighbours(estimate)
        beside = east_face * padded[2:, 1:-1] + west_face * padded[:-2, 1:-1]
        beside = beside + north_face * padded[1:-1, 2:] + south_face * padded[1:-1, :-2]
        estimate = estimate + RELAX * (forcing_head - (diagonal * estimate - beside)) / diagonal
    return estimate


def pad_zero(estimate):
    return jnp.pad(estimate, 1)


def reference(column_seed, head_seed, texture, soil_table, active, conductance, wells, transmissivity, storage):
    water_number = lookup(texture, soil_table[0])
    heat_number = lookup(texture, soil_table[1])
    coupling = 0.2 * lookup(texture, soil_table[2])
    water_faces = 0.5 * (water_number[:-1] + water_number[1:])
    heat_faces = 0.5 * (heat_number[:-1] + heat_number[1:])
    face_set = face_arrays(jnp.pad(transmissivity, 1), 0, 0, NX, NY)
    gain = jnp.where(active == 1, conductance, 0.0)
    col_ids = lax.broadcasted_iota(jnp.int32, (NX, NY), 1)
    well_rows = (wells // CY).astype(jnp.int32)
    well_cols = ((col_ids // CY) * CY + wells % CY).astype(jnp.int32)
    water_adjoint = column_seed[0]
    heat_adjoint = column_seed[1]
    head_state = head_seed
    recharge = jnp.zeros((NX, NY), jnp.float32)
    for time_step in range(STEPS):
        heat_next = column_solve(heat_faces, heat_adjoint)
        recharge = relax(head_state, face_set, storage, pad_zero)
        forcing = water_adjoint + coupling * heat_next
        forcing = jnp.concatenate([forcing[:-1], (forcing[-1] + gain * recharge)[None]], 0)
        water_next = column_solve(water_faces, forcing)
        well_term = gain * water_next[-1]
        well_sum = jnp.zeros((NX, NY), jnp.float32).at[well_rows, well_cols].add(well_term)
        head_state = recharge + well_sum
        water_adjoint = water_next
        heat_adjoint = heat_next
    return jnp.stack([water_adjoint, heat_adjoint]), recharge, head_state
```

```python
import jax
import jax.numpy as jnp
from jax import lax
from jax.sharding import PartitionSpec as P

SWEEPS = 4
STEPS = 2
HALO = SWEEPS

RELAX = 0.8


def aq_halo(block, width):
    count = lax.axis_size("aq")
    forward = [(i, i + 1) for i in range(count - 1)]
    backward = [(target, source) for source, target in forward]
    low = lax.ppermute(block[..., block.shape[-1] - width:], "aq", forward)
    high = lax.ppermute(block[..., :width], "aq", backward)
    return jnp.concatenate([low, block, high], axis=-1)


def lookup(texture, table_row):
    values = jnp.zeros(texture.shape, jnp.float32)
    for number in range(table_row.shape[0]):
        values = jnp.where(texture == number, table_row[number], values)
    return values


def column_solve(faces, forcing):
    layer_count = forcing.shape[0]
    ratios = []
    partials = []
    for layer_index in range(layer_count):
        diagonal = jnp.ones_like(forcing[0])
        if layer_index > 0:
            diagonal = diagonal + faces[layer_index - 1]
        if layer_index < layer_count - 1:
            diagonal = diagonal + faces[layer_index]
        if layer_index == 0:
            pivot_value = diagonal
            carried = forcing[0]
        else:
            pivot_value = diagonal - faces[layer_index - 1] * ratios[-1]
            carried = forcing[layer_index] + faces[layer_index - 1] * partials[-1]
        if layer_index < layer_count - 1:
            ratios.append(faces[layer_index] / pivot_value)
        partials.append(carried / pivot_value)
    solution = [partials[-1]]
    for layer_index in range(layer_count - 2, -1, -1):
        solution.append(partials[layer_index] + ratios[layer_index] * solution[-1])
    return jnp.stack(solution[::-1])


def relax(forcing_head, face_set, diagonal):
    east_face, west_face, north_face, south_face = face_set
    estimate = jnp.zeros_like(forcing_head)
    for sweep_number in range(SWEEPS):
        padded = jnp.pad(estimate, 1)
        beside = east_face * padded[2:, 1:-1] + west_face * padded[:-2, 1:-1]
        beside = beside + north_face * padded[1:-1, 2:] + south_face * padded[1:-1, :-2]
        estimate = estimate + RELAX * (forcing_head - (diagonal * estimate - beside)) / diagonal
    return estimate


def reduce_rows(slab, window, step):
    count = lax.axis_size("long")
    rows, cols = slab.shape
    edge = (window - step) // 2
    padded = jnp.pad(slab, ((edge, edge), (0, 0)))
    blocks = padded.reshape(-1, step, cols)
    parts = [blocks[k: k + count] for k in range(window // step)]
    chunks = jnp.stack(parts, axis=1).reshape(count, window, cols)
    got = lax.all_to_all(chunks, "long", 0, 0, tiled=True)
    return jnp.sum(got, axis=0)


def shards(
    column_seed, head_seed, texture, soil_table, active, conductance, wells, transmissivity, storage
):
    local_rows = column_seed.shape[2]
    local_cols = column_seed.shape[3]
    total_rows = local_rows * lax.axis_size("long")
    total_cols = local_cols * lax.axis_size("aq")
    row_start = lax.axis_index("long") * local_rows
    col_start = lax.axis_index("aq") * local_cols
    water_number = lookup(texture, soil_table[0])
    heat_number = lookup(texture, soil_table[1])
    coupling = 0.2 * lookup(texture, soil_table[2])
    water_faces = 0.5 * (water_number[:-1] + water_number[1:])
    heat_faces = 0.5 * (heat_number[:-1] + heat_number[1:])
    gain = jnp.where(active == 1, conductance, 0.0)

    fields = aq_halo(jnp.stack([head_seed, transmissivity, storage]), HALO)
    fields = jnp.pad(fields, ((0, 0), (HALO, HALO), (0, 0)))
    head_ext, trans_ext, storage_ext = fields[0], fields[1], fields[2]
    ext_rows, ext_cols = head_ext.shape
    row_ids = lax.broadcasted_iota(jnp.int32, (ext_rows, ext_cols), 0) - HALO
    col_ids = col_start - HALO + lax.broadcasted_iota(jnp.int32, (ext_rows, ext_cols), 1)
    valid = (row_ids >= 0) & (row_ids < total_rows) & (col_ids >= 0) & (col_ids < total_cols)
    tp = jnp.pad(trans_ext, 1)
    centre = tp[1:-1, 1:-1]
    east_face = jnp.where(valid & (row_ids + 1 < total_rows), 0.5 * (centre + tp[2:, 1:-1]), 0.0)
    west_face = jnp.where(valid & (row_ids >= 1), 0.5 * (centre + tp[:-2, 1:-1]), 0.0)
    north_face = jnp.where(valid & (col_ids + 1 < total_cols), 0.5 * (centre + tp[1:-1, 2:]), 0.0)
    south_face = jnp.where(valid & (col_ids >= 1), 0.5 * (centre + tp[1:-1, :-2]), 0.0)
    diagonal = storage_ext + east_face + west_face + north_face + south_face
    diagonal = jnp.where(valid, diagonal, 1.0)
    face_set = (east_face, west_face, north_face, south_face)

    window = local_rows + 2 * HALO

    def window_of(a):
        return lax.dynamic_slice_in_dim(a, row_start, window, 0)

    face_win = tuple(window_of(f) for f in face_set)
    diag_win = window_of(diagonal)

    flat_wells = wells.reshape(-1)

    def well_slab(water_bottom):
        well_term = gain * water_bottom
        owner_slab = (
            jnp.zeros((total_rows * local_cols,), jnp.float32)
            .at[flat_wells]
            .add(well_term.reshape(-1))
        )
        return owner_slab.reshape(total_rows, local_cols)

    core = slice(HALO, HALO + local_rows), slice(HALO, HALO + local_cols)

    heat_1 = column_solve(heat_faces, column_seed[1])
    estimate_1 = relax(head_ext, face_set, diagonal)
    recharge_1_win = window_of(estimate_1)[:, HALO:HALO + local_cols]
    recharge_1 = recharge_1_win[HALO:HALO + local_rows]
    forcing = column_seed[0] + coupling * heat_1
    forcing = jnp.concatenate([forcing[:-1], (forcing[-1] + gain * recharge_1)[None]], 0)
    water_1 = column_solve(water_faces, forcing)
    head_1_win = recharge_1_win + reduce_rows(well_slab(water_1[-1]), window, local_rows)

    heat_2 = column_solve(heat_faces, heat_1)
    head_1_ext = aq_halo(head_1_win, HALO)
    estimate_2 = relax(head_1_ext, face_win, diag_win)
    recharge_2 = estimate_2[core]
    forcing = water_1 + coupling * heat_2
    forcing = jnp.concatenate([forcing[:-1], (forcing[-1] + gain * recharge_2)[None]], 0)
    water_2 = column_solve(water_faces, forcing)
    head_2 = recharge_2 + reduce_rows(well_slab(water_2[-1]), local_rows, local_rows)
    return (jnp.stack([water_2, heat_2]), recharge_2, head_2)


def solution(mesh):
    return jax.shard_map(
        shards,
        mesh=mesh,
        in_specs=(
            P(None, None, "long", "aq"),
            P(None, "aq"),
            P(None, "long", "aq"),
            P(),
            P("long", "aq"),
            P("long", "aq"),
            P("long", "aq"),
            P(None, "aq"),
            P(None, "aq"),
        ),
        out_specs=(P(None, None, "long", "aq"), P("long", "aq"), P("long", "aq")),
        check_vma=False,
    )
```

```python
import functools

import jax
import jax.numpy as jnp
from jax import lax
from jax.experimental import pallas as pl
from jax.experimental.pallas import tpu as pltpu
from jax.sharding import PartitionSpec as P

MESH = pl.DeviceIdType.MESH

SWEEPS = 4
STEPS = 2
HALO = SWEEPS

RELAX = 0.8


def aq_halo(block, width):
    count = lax.axis_size("aq")
    forward = [(i, i + 1) for i in range(count - 1)]
    backward = [(target, source) for source, target in forward]
    low = lax.ppermute(block[..., block.shape[-1] - width:], "aq", forward)
    high = lax.ppermute(block[..., :width], "aq", backward)
    return jnp.concatenate([low, block, high], axis=-1)


def lookup(texture, table_row):
    values = jnp.zeros(texture.shape, jnp.float32)
    for number in range(table_row.shape[0]):
        values = jnp.where(texture == number, table_row[number], values)
    return values


def column_solve(faces, forcing):
    layer_count = forcing.shape[0]
    ratios = []
    partials = []
    for layer_index in range(layer_count):
        diagonal = jnp.ones_like(forcing[0])
        if layer_index > 0:
            diagonal = diagonal + faces[layer_index - 1]
        if layer_index < layer_count - 1:
            diagonal = diagonal + faces[layer_index]
        if layer_index == 0:
            pivot_value = diagonal
            carried = forcing[0]
        else:
            pivot_value = diagonal - faces[layer_index - 1] * ratios[-1]
            carried = forcing[layer_index] + faces[layer_index - 1] * partials[-1]
        if layer_index < layer_count - 1:
            ratios.append(faces[layer_index] / pivot_value)
        partials.append(carried / pivot_value)
    solution = [partials[-1]]
    for layer_index in range(layer_count - 2, -1, -1):
        solution.append(partials[layer_index] + ratios[layer_index] * solution[-1])
    return jnp.stack(solution[::-1])


def relax(forcing_head, face_set, diagonal):
    east_face, west_face, north_face, south_face = face_set
    estimate = jnp.zeros_like(forcing_head)
    for sweep_number in range(SWEEPS):
        padded = jnp.pad(estimate, 1)
        beside = east_face * padded[2:, 1:-1] + west_face * padded[:-2, 1:-1]
        beside = beside + north_face * padded[1:-1, 2:] + south_face * padded[1:-1, :-2]
        estimate = estimate + RELAX * (forcing_head - (diagonal * estimate - beside)) / diagonal
    return estimate


def exchange_kernel(count, chunks_ref, out_ref, recv, send_sem, recv_sem):
    me = lax.axis_index("long")
    column = lax.axis_index("aq")
    barrier = pltpu.get_barrier_semaphore()
    for k in range(1, count):
        pl.semaphore_signal(
            barrier, inc=1, device_id=(lax.rem(me + k, count), column), device_id_type=MESH
        )
    pl.semaphore_wait(barrier, count - 1)
    copies = []
    for k in range(1, count):
        peer = lax.rem(me + k, count)
        copy = pltpu.make_async_remote_copy(
            src_ref=chunks_ref.at[peer],
            dst_ref=recv.at[k],
            send_sem=send_sem.at[k],
            recv_sem=recv_sem.at[k],
            device_id=(peer, column),
            device_id_type=MESH,
        )
        copy.start()
        copies.append(copy)
    total = chunks_ref[me]
    for k in range(1, count):
        copies[k - 1].wait()
        total = total + recv[k]
    out_ref[...] = total


def reduce_rows(slab, window, step, collective_id):
    count = lax.axis_size("long")
    rows, cols = slab.shape
    edge = (window - step) // 2
    padded = jnp.pad(slab, ((edge, edge), (0, 0)))
    blocks = padded.reshape(-1, step, cols)
    parts = [blocks[k: k + count] for k in range(window // step)]
    chunks = jnp.stack(parts, axis=1).reshape(count, window, cols)
    return pl.pallas_call(
        functools.partial(exchange_kernel, count),
        out_shape=jax.ShapeDtypeStruct((window, cols), jnp.float32),
        in_specs=[pl.BlockSpec(memory_space=pltpu.VMEM)],
        out_specs=pl.BlockSpec(memory_space=pltpu.VMEM),
        scratch_shapes=[
            pltpu.VMEM((count, window, cols), jnp.float32),
            pltpu.SemaphoreType.DMA((count,)),
            pltpu.SemaphoreType.DMA((count,)),
        ],
        compiler_params=pltpu.CompilerParams(collective_id=collective_id, has_side_effects=True),
    )(chunks)


def shards(
    column_seed, head_seed, texture, soil_table, active, conductance, wells, transmissivity, storage
):
    local_rows = column_seed.shape[2]
    local_cols = column_seed.shape[3]
    total_rows = local_rows * lax.axis_size("long")
    total_cols = local_cols * lax.axis_size("aq")
    row_start = lax.axis_index("long") * local_rows
    col_start = lax.axis_index("aq") * local_cols
    water_number = lookup(texture, soil_table[0])
    heat_number = lookup(texture, soil_table[1])
    coupling = 0.2 * lookup(texture, soil_table[2])
    water_faces = 0.5 * (water_number[:-1] + water_number[1:])
    heat_faces = 0.5 * (heat_number[:-1] + heat_number[1:])
    gain = jnp.where(active == 1, conductance, 0.0)

    fields = aq_halo(jnp.stack([head_seed, transmissivity, storage]), HALO)
    fields = jnp.pad(fields, ((0, 0), (HALO, HALO), (0, 0)))
    head_ext, trans_ext, storage_ext = fields[0], fields[1], fields[2]
    ext_rows, ext_cols = head_ext.shape
    row_ids = lax.broadcasted_iota(jnp.int32, (ext_rows, ext_cols), 0) - HALO
    col_ids = col_start - HALO + lax.broadcasted_iota(jnp.int32, (ext_rows, ext_cols), 1)
    valid = (row_ids >= 0) & (row_ids < total_rows) & (col_ids >= 0) & (col_ids < total_cols)
    tp = jnp.pad(trans_ext, 1)
    centre = tp[1:-1, 1:-1]
    east_face = jnp.where(valid & (row_ids + 1 < total_rows), 0.5 * (centre + tp[2:, 1:-1]), 0.0)
    west_face = jnp.where(valid & (row_ids >= 1), 0.5 * (centre + tp[:-2, 1:-1]), 0.0)
    north_face = jnp.where(valid & (col_ids + 1 < total_cols), 0.5 * (centre + tp[1:-1, 2:]), 0.0)
    south_face = jnp.where(valid & (col_ids >= 1), 0.5 * (centre + tp[1:-1, :-2]), 0.0)
    diagonal = storage_ext + east_face + west_face + north_face + south_face
    diagonal = jnp.where(valid, diagonal, 1.0)
    face_set = (east_face, west_face, north_face, south_face)

    window = local_rows + 2 * HALO

    def window_of(a):
        return lax.dynamic_slice_in_dim(a, row_start, window, 0)

    face_win = tuple(window_of(f) for f in face_set)
    diag_win = window_of(diagonal)

    flat_wells = wells.reshape(-1)

    def well_slab(water_bottom):
        well_term = gain * water_bottom
        owner_slab = (
            jnp.zeros((total_rows * local_cols,), jnp.float32)
            .at[flat_wells]
            .add(well_term.reshape(-1))
        )
        return owner_slab.reshape(total_rows, local_cols)

    core = slice(HALO, HALO + local_rows), slice(HALO, HALO + local_cols)

    heat_1 = column_solve(heat_faces, column_seed[1])
    estimate_1 = relax(head_ext, face_set, diagonal)
    recharge_1_win = window_of(estimate_1)[:, HALO:HALO + local_cols]
    recharge_1 = recharge_1_win[HALO:HALO + local_rows]
    forcing = column_seed[0] + coupling * heat_1
    forcing = jnp.concatenate([forcing[:-1], (forcing[-1] + gain * recharge_1)[None]], 0)
    water_1 = column_solve(water_faces, forcing)
    head_1_win = recharge_1_win + reduce_rows(well_slab(water_1[-1]), window, local_rows, 0)

    heat_2 = column_solve(heat_faces, heat_1)
    head_1_ext = aq_halo(head_1_win, HALO)
    estimate_2 = relax(head_1_ext, face_win, diag_win)
    recharge_2 = estimate_2[core]
    forcing = water_1 + coupling * heat_2
    forcing = jnp.concatenate([forcing[:-1], (forcing[-1] + gain * recharge_2)[None]], 0)
    water_2 = column_solve(water_faces, forcing)
    head_2 = recharge_2 + reduce_rows(well_slab(water_2[-1]), local_rows, local_rows, 1)
    return (jnp.stack([water_2, heat_2]), recharge_2, head_2)


def solution(mesh):
    return jax.shard_map(
        shards,
        mesh=mesh,
        in_specs=(
            P(None, None, "long", "aq"),
            P(None, "aq"),
            P(None, "long", "aq"),
            P(),
            P("long", "aq"),
            P("long", "aq"),
            P("long", "aq"),
            P(None, "aq"),
            P(None, "aq"),
        ),
        out_specs=(P(None, None, "long", "aq"), P("long", "aq"), P("long", "aq")),
        check_vma=False,
    )
```

```python
import functools

import jax
import jax.numpy as jnp
from jax import lax
from jax.experimental import pallas as pl
from jax.experimental.pallas import tpu as pltpu
from jax.sharding import PartitionSpec as P

MESH = pl.DeviceIdType.MESH

SWEEPS = 4
STEPS = 2
HALO = SWEEPS

RELAX = 0.8


def aq_halo(block, width):
    count = lax.axis_size("aq")
    forward = [(i, i + 1) for i in range(count - 1)]
    backward = [(target, source) for source, target in forward]
    low = lax.ppermute(block[..., block.shape[-1] - width:], "aq", forward)
    high = lax.ppermute(block[..., :width], "aq", backward)
    return jnp.concatenate([low, block, high], axis=-1)


def column_kernel(
    table, tex, seed, heat_1, heat_2, c_out, d_out, b_out, a_last,
    wnum, hnum, coup, wface, hface, wratio, wpivot, hratio, hpivot, part_a, part_b, part_c, a_sol,
):
    layers = tex.shape[0]
    classes = table.shape[1]
    for l in range(layers):
        t = tex[l]
        w = jnp.zeros(t.shape, jnp.float32)
        h = jnp.zeros(t.shape, jnp.float32)
        c = jnp.zeros(t.shape, jnp.float32)
        for k in range(classes):
            m = t == k
            w = jnp.where(m, table[0, k], w)
            h = jnp.where(m, table[1, k], h)
            c = jnp.where(m, table[2, k], c)
        wnum[l] = w
        hnum[l] = h
        coup[l] = 0.2 * c
    for l in range(layers - 1):
        wface[l] = 0.5 * (wnum[l] + wnum[l + 1])
        hface[l] = 0.5 * (hnum[l] + hnum[l + 1])

    def factor(l, face, ratio, pivot, prev):
        diagonal = jnp.ones(tex.shape[1:], jnp.float32)
        if l > 0:
            diagonal = diagonal + face[l - 1]
        if l < layers - 1:
            diagonal = diagonal + face[l]
        p = diagonal if l == 0 else diagonal - face[l - 1] * prev
        pivot[l] = p
        if l < layers - 1:
            r = face[l] / p
            ratio[l] = r
            return r
        return None

    def forward(l, face, pivot, forcing, part, prev):
        carried = forcing if l == 0 else forcing + face[l - 1] * prev
        value = carried / pivot[l]
        part[l] = value
        return value

    def backward(l, ratio, part, out, prev):
        value = part[l] if l == layers - 1 else part[l] + ratio[l] * prev
        out[l] = value
        return value

    wr = hr = hp = None
    for l in range(layers):
        wr = factor(l, wface, wratio, wpivot, wr)
        hr = factor(l, hface, hratio, hpivot, hr)
        hp = forward(l, hface, hpivot, seed[1, l], part_a, hp)
    h1 = b = None
    for l in range(layers - 1, -1, -1):
        h1 = backward(l, hratio, part_a, heat_1, h1)
        b = 1.0 / wpivot[l] if l == layers - 1 else wratio[l] * b
        b_out[l] = b
    hp = ap = dp = None
    for l in range(layers):
        hp = forward(l, hface, hpivot, heat_1[l], part_a, hp)
        ap = forward(l, wface, wpivot, seed[0, l] + coup[l] * heat_1[l], part_b, ap)
        dp = forward(l, wface, wpivot, b_out[l], part_c, dp)
    a_last[...] = ap
    h2 = a = d = None
    for l in range(layers - 1, -1, -1):
        h2 = backward(l, hratio, part_a, heat_2, h2)
        a = backward(l, wratio, part_b, a_sol, a)
        d = backward(l, wratio, part_c, d_out, d)
    cp = None
    for l in range(layers):
        cp = forward(l, wface, wpivot, a_sol[l] + coup[l] * heat_2[l], part_b, cp)
    c = None
    for l in range(layers - 1, -1, -1):
        c = backward(l, wratio, part_b, c_out, c)


def column_solves(soil_table, texture, column_seed):
    layers, rows, cols = texture.shape
    full = jax.ShapeDtypeStruct((layers, rows, cols), jnp.float32)
    vmem = pl.BlockSpec(memory_space=pltpu.VMEM)
    return pl.pallas_call(
        column_kernel,
        out_shape=(full, full, full, full, full, jax.ShapeDtypeStruct((rows, cols), jnp.float32)),
        in_specs=[pl.BlockSpec(memory_space=pltpu.SMEM), vmem, vmem],
        out_specs=(vmem,) * 6,
        scratch_shapes=[pltpu.VMEM((layers, rows, cols), jnp.float32)] * 13,
    )(soil_table, texture, column_seed)


def relax(forcing_head, face_set, diagonal):
    east_face, west_face, north_face, south_face = face_set
    estimate = jnp.zeros_like(forcing_head)
    for sweep_number in range(SWEEPS):
        padded = jnp.pad(estimate, 1)
        beside = east_face * padded[2:, 1:-1] + west_face * padded[:-2, 1:-1]
        beside = beside + north_face * padded[1:-1, 2:] + south_face * padded[1:-1, :-2]
        estimate = estimate + RELAX * (forcing_head - (diagonal * estimate - beside)) / diagonal
    return estimate


def exchange_kernel(count, chunks_ref, out_ref, recv, send_sem, recv_sem):
    me = lax.axis_index("long")
    column = lax.axis_index("aq")
    barrier = pltpu.get_barrier_semaphore()
    for k in range(1, count):
        pl.semaphore_signal(
            barrier, inc=1, device_id=(lax.rem(me + k, count), column), device_id_type=MESH
        )
    pl.semaphore_wait(barrier, count - 1)
    copies = []
    for k in range(1, count):
        peer = lax.rem(me + k, count)
        copy = pltpu.make_async_remote_copy(
            src_ref=chunks_ref.at[peer],
            dst_ref=recv.at[k],
            send_sem=send_sem.at[k],
            recv_sem=recv_sem.at[k],
            device_id=(peer, column),
            device_id_type=MESH,
        )
        copy.start()
        copies.append(copy)
    total = chunks_ref[me]
    for k in range(1, count):
        copies[k - 1].wait()
        total = total + recv[k]
    out_ref[...] = total


def reduce_rows(term, wells, window, step, collective_id):
    count = lax.axis_size("long")
    cols = term.shape[1]
    edge = (window - step) // 2
    flat_wells = wells.reshape(1, -1)
    slot = lax.broadcasted_iota(jnp.int32, (count * window, 1), 0)
    target_row = (slot // window) * step - edge + slot % window
    spread = jnp.where(flat_wells // cols == target_row, term.reshape(1, -1), 0.0)
    picks = flat_wells.reshape(-1, 1) % cols == lax.broadcasted_iota(jnp.int32, (1, cols), 1)
    chunks = jnp.dot(spread, picks.astype(jnp.float32), precision=lax.Precision.HIGHEST)
    chunks = chunks.reshape(count, window, cols)
    return pl.pallas_call(
        functools.partial(exchange_kernel, count),
        out_shape=jax.ShapeDtypeStruct((window, cols), jnp.float32),
        in_specs=[pl.BlockSpec(memory_space=pltpu.VMEM)],
        out_specs=pl.BlockSpec(memory_space=pltpu.VMEM),
        scratch_shapes=[
            pltpu.VMEM((count, window, cols), jnp.float32),
            pltpu.SemaphoreType.DMA((count,)),
            pltpu.SemaphoreType.DMA((count,)),
        ],
        compiler_params=pltpu.CompilerParams(collective_id=collective_id, has_side_effects=True),
    )(chunks)


def shards(
    column_seed, head_seed, texture, soil_table, active, conductance, wells, transmissivity, storage
):
    local_rows = column_seed.shape[2]
    local_cols = column_seed.shape[3]
    total_rows = local_rows * lax.axis_size("long")
    total_cols = local_cols * lax.axis_size("aq")
    row_start = lax.axis_index("long") * local_rows
    col_start = lax.axis_index("aq") * local_cols
    heat_1, heat_2, c_sol, d_sol, b_sol, a_last = column_solves(soil_table, texture, column_seed)
    gain = jnp.where(active == 1, conductance, 0.0)

    fields = aq_halo(jnp.stack([head_seed, transmissivity, storage]), HALO)
    fields = jnp.pad(fields, ((0, 0), (HALO, HALO), (0, 0)))
    head_ext, trans_ext, storage_ext = fields[0], fields[1], fields[2]
    ext_rows, ext_cols = head_ext.shape
    row_ids = lax.broadcasted_iota(jnp.int32, (ext_rows, ext_cols), 0) - HALO
    col_ids = col_start - HALO + lax.broadcasted_iota(jnp.int32, (ext_rows, ext_cols), 1)
    valid = (row_ids >= 0) & (row_ids < total_rows) & (col_ids >= 0) & (col_ids < total_cols)
    tp = jnp.pad(trans_ext, 1)
    centre = tp[1:-1, 1:-1]
    east_face = jnp.where(valid & (row_ids + 1 < total_rows), 0.5 * (centre + tp[2:, 1:-1]), 0.0)
    west_face = jnp.where(valid & (row_ids >= 1), 0.5 * (centre + tp[:-2, 1:-1]), 0.0)
    north_face = jnp.where(valid & (col_ids + 1 < total_cols), 0.5 * (centre + tp[1:-1, 2:]), 0.0)
    south_face = jnp.where(valid & (col_ids >= 1), 0.5 * (centre + tp[1:-1, :-2]), 0.0)
    diagonal = storage_ext + east_face + west_face + north_face + south_face
    diagonal = jnp.where(valid, diagonal, 1.0)
    face_set = (east_face, west_face, north_face, south_face)

    window = local_rows + 2 * HALO

    def window_of(a):
        return lax.dynamic_slice_in_dim(a, row_start, window, 0)

    face_win = tuple(window_of(f) for f in face_set)
    diag_win = window_of(diagonal)
    core = slice(HALO, HALO + local_rows), slice(HALO, HALO + local_cols)

    estimate_1 = relax(head_ext, face_set, diagonal)
    recharge_1_win = window_of(estimate_1)[:, HALO:HALO + local_cols]
    recharge_1 = recharge_1_win[HALO:HALO + local_rows]
    r_1 = gain * recharge_1
    term_1 = gain * (a_last + r_1 * b_sol[-1])
    head_1_win = recharge_1_win + reduce_rows(term_1, wells, window, local_rows, 0)

    head_1_ext = aq_halo(head_1_win, HALO)
    estimate_2 = relax(head_1_ext, face_win, diag_win)
    recharge_2 = estimate_2[core]
    r_2 = gain * recharge_2
    term_2 = gain * (c_sol[-1] + r_1 * d_sol[-1] + r_2 * b_sol[-1])
    head_2 = recharge_2 + reduce_rows(term_2, wells, local_rows, local_rows, 1)
    water_2 = c_sol + r_1 * d_sol + r_2 * b_sol
    return (jnp.stack([water_2, heat_2]), recharge_2, head_2)


def solution(mesh):
    return jax.shard_map(
        shards,
        mesh=mesh,
        in_specs=(
            P(None, None, "long", "aq"),
            P(None, "aq"),
            P(None, "long", "aq"),
            P(),
            P("long", "aq"),
            P("long", "aq"),
            P("long", "aq"),
            P(None, "aq"),
            P(None, "aq"),
        ),
        out_specs=(P(None, None, "long", "aq"), P("long", "aq"), P("long", "aq")),
        check_vma=False,
    )
```

```python
import functools

import jax
import jax.numpy as jnp
from jax import lax
from jax.experimental import pallas as pl
from jax.experimental.pallas import tpu as pltpu
from jax.sharding import PartitionSpec as P

MESH = pl.DeviceIdType.MESH

SWEEPS = 4
STEPS = 2
HALO = SWEEPS

RELAX = 0.8


def aq_halo(block, width):
    count = lax.axis_size("aq")
    forward = [(i, i + 1) for i in range(count - 1)]
    backward = [(target, source) for source, target in forward]
    low = lax.ppermute(jnp.swapaxes(block[..., block.shape[-1] - width:], -1, -2), "aq", forward)
    high = lax.ppermute(jnp.swapaxes(block[..., :width], -1, -2), "aq", backward)
    return jnp.concatenate(
        [jnp.swapaxes(low, -1, -2), block, jnp.swapaxes(high, -1, -2)], axis=-1
    )


def column_kernel(
    table, tex, seed, heat_1, heat_2, c_out, d_out, b_out, a_last,
    wnum, hnum, coup, wface, hface, wratio, wpivot, hratio, hpivot, part_a, part_b, part_c, a_sol,
):
    layers = tex.shape[0]
    classes = table.shape[1]
    for l in range(layers):
        t = tex[l]
        w = jnp.zeros(t.shape, jnp.float32)
        h = jnp.zeros(t.shape, jnp.float32)
        c = jnp.zeros(t.shape, jnp.float32)
        for k in range(classes):
            m = t == k
            w = jnp.where(m, table[0, k], w)
            h = jnp.where(m, table[1, k], h)
            c = jnp.where(m, table[2, k], c)
        wnum[l] = w
        hnum[l] = h
        coup[l] = 0.2 * c
    for l in range(layers - 1):
        wface[l] = 0.5 * (wnum[l] + wnum[l + 1])
        hface[l] = 0.5 * (hnum[l] + hnum[l + 1])

    def factor(l, face, ratio, pivot, prev):
        diagonal = jnp.ones(tex.shape[1:], jnp.float32)
        if l > 0:
            diagonal = diagonal + face[l - 1]
        if l < layers - 1:
            diagonal = diagonal + face[l]
        p = diagonal if l == 0 else diagonal - face[l - 1] * prev
        pivot[l] = p
        if l < layers - 1:
            r = face[l] / p
            ratio[l] = r
            return r
        return None

    def forward(l, face, pivot, forcing, part, prev):
        carried = forcing if l == 0 else forcing + face[l - 1] * prev
        value = carried / pivot[l]
        part[l] = value
        return value

    def backward(l, ratio, part, out, prev):
        value = part[l] if l == layers - 1 else part[l] + ratio[l] * prev
        out[l] = value
        return value

    wr = hr = hp = None
    for l in range(layers):
        wr = factor(l, wface, wratio, wpivot, wr)
        hr = factor(l, hface, hratio, hpivot, hr)
        hp = forward(l, hface, hpivot, seed[1, l], part_a, hp)
    h1 = b = None
    for l in range(layers - 1, -1, -1):
        h1 = backward(l, hratio, part_a, heat_1, h1)
        b = 1.0 / wpivot[l] if l == layers - 1 else wratio[l] * b
        b_out[l] = b
    hp = ap = dp = None
    for l in range(layers):
        hp = forward(l, hface, hpivot, heat_1[l], part_a, hp)
        ap = forward(l, wface, wpivot, seed[0, l] + coup[l] * heat_1[l], part_b, ap)
        dp = forward(l, wface, wpivot, b_out[l], part_c, dp)
    a_last[...] = ap
    h2 = a = d = None
    for l in range(layers - 1, -1, -1):
        h2 = backward(l, hratio, part_a, heat_2, h2)
        a = backward(l, wratio, part_b, a_sol, a)
        d = backward(l, wratio, part_c, d_out, d)
    cp = None
    for l in range(layers):
        cp = forward(l, wface, wpivot, a_sol[l] + coup[l] * heat_2[l], part_b, cp)
    c = None
    for l in range(layers - 1, -1, -1):
        c = backward(l, wratio, part_b, c_out, c)


def column_solves(soil_table, texture, column_seed):
    layers, rows, cols = texture.shape
    full = jax.ShapeDtypeStruct((layers, rows, cols), jnp.float32)
    vmem = pl.BlockSpec(memory_space=pltpu.VMEM)
    return pl.pallas_call(
        column_kernel,
        out_shape=(full, full, full, full, full, jax.ShapeDtypeStruct((rows, cols), jnp.float32)),
        in_specs=[pl.BlockSpec(memory_space=pltpu.SMEM), vmem, vmem],
        out_specs=(vmem,) * 6,
        scratch_shapes=[pltpu.VMEM((layers, rows, cols), jnp.float32)] * 13,
    )(soil_table, texture, column_seed)


def relax(forcing_head, face_set, diagonal):
    east_face, west_face, north_face, south_face = face_set
    estimate = jnp.zeros_like(forcing_head)
    for sweep_number in range(SWEEPS):
        padded = jnp.pad(estimate, 1)
        beside = east_face * padded[2:, 1:-1] + west_face * padded[:-2, 1:-1]
        beside = beside + north_face * padded[1:-1, 2:] + south_face * padded[1:-1, :-2]
        estimate = estimate + RELAX * (forcing_head - (diagonal * estimate - beside)) / diagonal
    return estimate


def exchange_kernel(planes, chunks_ref, out_ref, partial, recv_a, recv_b, send_a, got_a, send_b, got_b):
    groups = chunks_ref.shape[0]
    me = lax.axis_index("long")
    column = lax.axis_index("aq")
    my_core = lax.rem(me, 2)
    my_plane = lax.rem(me // 2, planes)
    my_group = (me // (2 * planes)) * 2 + my_core

    def long_of(group, plane):
        return (group // 2) * (2 * planes) + 2 * plane + lax.rem(group, 2)

    peers_a = [long_of(lax.rem(my_group + k, groups), my_plane) for k in range(1, groups)]
    peers_b = [long_of(my_group, lax.rem(my_plane + k, planes)) for k in range(1, planes)]
    barrier = pltpu.get_barrier_semaphore()
    for peer in peers_a + peers_b:
        pl.semaphore_signal(barrier, inc=1, device_id=(peer, column), device_id_type=MESH)
    pl.semaphore_wait(barrier, len(peers_a) + len(peers_b))
    copies = []
    for k in range(1, groups):
        copy = pltpu.make_async_remote_copy(
            src_ref=chunks_ref.at[lax.rem(my_group + k, groups)],
            dst_ref=recv_a.at[k],
            send_sem=send_a.at[k],
            recv_sem=got_a.at[k],
            device_id=(peers_a[k - 1], column),
            device_id_type=MESH,
        )
        copy.start()
        copies.append(copy)
    acc = chunks_ref[my_group]
    for k in range(1, groups):
        copies[k - 1].wait()
        acc = acc + recv_a[k]
    partial[...] = acc
    copies = []
    for k in range(1, planes):
        copy = pltpu.make_async_remote_copy(
            src_ref=partial.at[lax.rem(my_plane + k, planes)],
            dst_ref=recv_b.at[k],
            send_sem=send_b.at[k],
            recv_sem=got_b.at[k],
            device_id=(peers_b[k - 1], column),
            device_id_type=MESH,
        )
        copy.start()
        copies.append(copy)
    total = partial[my_plane]
    for k in range(1, planes):
        copies[k - 1].wait()
        total = total + recv_b[k]
    out_ref[...] = total


PLANES = 4


def reduce_rows(term, wells, window, step, collective_id):
    count = lax.axis_size("long")
    planes = PLANES
    groups = count // planes
    cols = term.shape[1]
    edge = (window - step) // 2
    flat_wells = wells.reshape(1, -1)
    slot = lax.broadcasted_iota(jnp.int32, (count * window, 1), 0)
    group = slot // (planes * window)
    plane = (slot // window) % planes
    owner = (group // 2) * (2 * planes) + 2 * plane + group % 2
    target_row = owner * step - edge + slot % window
    spread = jnp.where(flat_wells // cols == target_row, term.reshape(1, -1), 0.0)
    picks = flat_wells.reshape(-1, 1) % cols == lax.broadcasted_iota(jnp.int32, (1, cols), 1)
    chunks = jnp.dot(spread, picks.astype(jnp.float32), precision=lax.Precision.HIGHEST)
    chunks = chunks.reshape(groups, planes, window, cols)
    return pl.pallas_call(
        functools.partial(exchange_kernel, planes),
        out_shape=jax.ShapeDtypeStruct((window, cols), jnp.float32),
        in_specs=[pl.BlockSpec(memory_space=pltpu.VMEM)],
        out_specs=pl.BlockSpec(memory_space=pltpu.VMEM),
        scratch_shapes=[
            pltpu.VMEM((planes, window, cols), jnp.float32),
            pltpu.VMEM((groups, planes, window, cols), jnp.float32),
            pltpu.VMEM((planes, window, cols), jnp.float32),
            pltpu.SemaphoreType.DMA((groups,)),
            pltpu.SemaphoreType.DMA((groups,)),
            pltpu.SemaphoreType.DMA((planes,)),
            pltpu.SemaphoreType.DMA((planes,)),
        ],
        compiler_params=pltpu.CompilerParams(collective_id=collective_id, has_side_effects=True),
    )(chunks)


def shards(
    column_seed, head_seed, texture, soil_table, active, conductance, wells, transmissivity, storage
):
    local_rows = column_seed.shape[2]
    local_cols = column_seed.shape[3]
    total_rows = local_rows * lax.axis_size("long")
    total_cols = local_cols * lax.axis_size("aq")
    row_start = lax.axis_index("long") * local_rows
    col_start = lax.axis_index("aq") * local_cols
    heat_1, heat_2, c_sol, d_sol, b_sol, a_last = column_solves(soil_table, texture, column_seed)
    gain = jnp.where(active == 1, conductance, 0.0)

    fields = aq_halo(jnp.stack([head_seed, transmissivity, storage]), HALO)
    fields = jnp.pad(fields, ((0, 0), (HALO, HALO), (0, 0)))
    head_ext, trans_ext, storage_ext = fields[0], fields[1], fields[2]
    ext_rows, ext_cols = head_ext.shape
    row_ids = lax.broadcasted_iota(jnp.int32, (ext_rows, ext_cols), 0) - HALO
    col_ids = col_start - HALO + lax.broadcasted_iota(jnp.int32, (ext_rows, ext_cols), 1)
    valid = (row_ids >= 0) & (row_ids < total_rows) & (col_ids >= 0) & (col_ids < total_cols)
    tp = jnp.pad(trans_ext, 1)
    centre = tp[1:-1, 1:-1]
    east_face = jnp.where(valid & (row_ids + 1 < total_rows), 0.5 * (centre + tp[2:, 1:-1]), 0.0)
    west_face = jnp.where(valid & (row_ids >= 1), 0.5 * (centre + tp[:-2, 1:-1]), 0.0)
    north_face = jnp.where(valid & (col_ids + 1 < total_cols), 0.5 * (centre + tp[1:-1, 2:]), 0.0)
    south_face = jnp.where(valid & (col_ids >= 1), 0.5 * (centre + tp[1:-1, :-2]), 0.0)
    diagonal = storage_ext + east_face + west_face + north_face + south_face
    diagonal = jnp.where(valid, diagonal, 1.0)
    face_set = (east_face, west_face, north_face, south_face)

    window = local_rows + 2 * HALO

    def window_of(a):
        return lax.dynamic_slice_in_dim(a, row_start, window, 0)

    face_win = tuple(window_of(f) for f in face_set)
    diag_win = window_of(diagonal)
    core = slice(HALO, HALO + local_rows), slice(HALO, HALO + local_cols)

    estimate_1 = relax(head_ext, face_set, diagonal)
    recharge_1_win = window_of(estimate_1)[:, HALO:HALO + local_cols]
    recharge_1 = recharge_1_win[HALO:HALO + local_rows]
    r_1 = gain * recharge_1
    term_1 = gain * (a_last + r_1 * b_sol[-1])
    head_1_win = recharge_1_win + reduce_rows(term_1, wells, window, local_rows, 0)

    head_1_ext = aq_halo(head_1_win, HALO)
    estimate_2 = relax(head_1_ext, face_win, diag_win)
    recharge_2 = estimate_2[core]
    r_2 = gain * recharge_2
    term_2 = gain * (c_sol[-1] + r_1 * d_sol[-1] + r_2 * b_sol[-1])
    head_2 = recharge_2 + reduce_rows(term_2, wells, local_rows, local_rows, 1)
    water_2 = c_sol + r_1 * d_sol + r_2 * b_sol
    return (jnp.stack([water_2, heat_2]), recharge_2, head_2)


def solution(mesh):
    return jax.shard_map(
        shards,
        mesh=mesh,
        in_specs=(
            P(None, None, "long", "aq"),
            P(None, "aq"),
            P(None, "long", "aq"),
            P(),
            P("long", "aq"),
            P("long", "aq"),
            P("long", "aq"),
            P(None, "aq"),
            P(None, "aq"),
        ),
        out_specs=(P(None, None, "long", "aq"), P("long", "aq"), P("long", "aq")),
        check_vma=False,
    )
```

```python
import functools

import jax
import jax.numpy as jnp
from jax import lax
from jax.experimental import pallas as pl
from jax.experimental.pallas import tpu as pltpu
from jax.sharding import PartitionSpec as P

MESH = pl.DeviceIdType.MESH

SWEEPS = 4
STEPS = 2
HALO = SWEEPS

RELAX = 0.8


def aq_halo(block, width):
    count = lax.axis_size("aq")
    forward = [(i, i + 1) for i in range(count - 1)]
    backward = [(target, source) for source, target in forward]
    low = lax.ppermute(jnp.swapaxes(block[..., block.shape[-1] - width:], -1, -2), "aq", forward)
    high = lax.ppermute(jnp.swapaxes(block[..., :width], -1, -2), "aq", backward)
    return jnp.concatenate(
        [jnp.swapaxes(low, -1, -2), block, jnp.swapaxes(high, -1, -2)], axis=-1
    )


def column_kernel(
    table, tex, seed, heat_1, heat_2, c_out, d_out, b_out, a_last,
    wnum, hnum, coup, wface, hface, wratio, wpivot, hratio, hpivot, part_a, part_b, part_c, a_sol,
):
    layers = tex.shape[0]
    classes = table.shape[1]
    for l in range(layers):
        t = tex[l]
        w = jnp.zeros(t.shape, jnp.float32)
        h = jnp.zeros(t.shape, jnp.float32)
        c = jnp.zeros(t.shape, jnp.float32)
        for k in range(classes):
            m = t == k
            w = jnp.where(m, table[0, k], w)
            h = jnp.where(m, table[1, k], h)
            c = jnp.where(m, table[2, k], c)
        wnum[l] = w
        hnum[l] = h
        coup[l] = 0.2 * c
    for l in range(layers - 1):
        wface[l] = 0.5 * (wnum[l] + wnum[l + 1])
        hface[l] = 0.5 * (hnum[l] + hnum[l + 1])

    def factor(l, face, ratio, pivot, prev):
        diagonal = jnp.ones(tex.shape[1:], jnp.float32)
        if l > 0:
            diagonal = diagonal + face[l - 1]
        if l < layers - 1:
            diagonal = diagonal + face[l]
        p = diagonal if l == 0 else diagonal - face[l - 1] * prev
        pivot[l] = p
        if l < layers - 1:
            r = face[l] / p
            ratio[l] = r
            return r
        return None

    def forward(l, face, pivot, forcing, part, prev):
        carried = forcing if l == 0 else forcing + face[l - 1] * prev
        value = carried / pivot[l]
        part[l] = value
        return value

    def backward(l, ratio, part, out, prev):
        value = part[l] if l == layers - 1 else part[l] + ratio[l] * prev
        out[l] = value
        return value

    wr = hr = hp = None
    for l in range(layers):
        wr = factor(l, wface, wratio, wpivot, wr)
        hr = factor(l, hface, hratio, hpivot, hr)
        hp = forward(l, hface, hpivot, seed[1, l], part_a, hp)
    h1 = b = None
    for l in range(layers - 1, -1, -1):
        h1 = backward(l, hratio, part_a, heat_1, h1)
        b = 1.0 / wpivot[l] if l == layers - 1 else wratio[l] * b
        b_out[l] = b
    hp = ap = dp = None
    for l in range(layers):
        hp = forward(l, hface, hpivot, heat_1[l], part_a, hp)
        ap = forward(l, wface, wpivot, seed[0, l] + coup[l] * heat_1[l], part_b, ap)
        dp = forward(l, wface, wpivot, b_out[l], part_c, dp)
    a_last[...] = ap
    h2 = a = d = None
    for l in range(layers - 1, -1, -1):
        h2 = backward(l, hratio, part_a, heat_2, h2)
        a = backward(l, wratio, part_b, a_sol, a)
        d = backward(l, wratio, part_c, d_out, d)
    cp = None
    for l in range(layers):
        cp = forward(l, wface, wpivot, a_sol[l] + coup[l] * heat_2[l], part_b, cp)
    c = None
    for l in range(layers - 1, -1, -1):
        c = backward(l, wratio, part_b, c_out, c)


def column_solves(soil_table, texture, column_seed):
    layers, rows, cols = texture.shape
    full = jax.ShapeDtypeStruct((layers, rows, cols), jnp.float32)
    vmem = pl.BlockSpec(memory_space=pltpu.VMEM)
    return pl.pallas_call(
        column_kernel,
        out_shape=(full, full, full, full, full, jax.ShapeDtypeStruct((rows, cols), jnp.float32)),
        in_specs=[pl.BlockSpec(memory_space=pltpu.SMEM), vmem, vmem],
        out_specs=(vmem,) * 6,
        scratch_shapes=[pltpu.VMEM((layers, rows, cols), jnp.float32)] * 13,
    )(soil_table, texture, column_seed)


def relax(forcing_head, face_set, diagonal):
    east_face, west_face, north_face, south_face = face_set
    estimate = jnp.zeros_like(forcing_head)
    for sweep_number in range(SWEEPS):
        padded = jnp.pad(estimate, 1)
        beside = east_face * padded[2:, 1:-1] + west_face * padded[:-2, 1:-1]
        beside = beside + north_face * padded[1:-1, 2:] + south_face * padded[1:-1, :-2]
        estimate = estimate + RELAX * (forcing_head - (diagonal * estimate - beside)) / diagonal
    return estimate


def exchange_kernel(planes, chunks_ref, out_ref, partial, recv_a, recv_b, send_a, got_a, send_b, got_b):
    groups = chunks_ref.shape[0]
    me = lax.axis_index("long")
    column = lax.axis_index("aq")
    my_core = lax.rem(me, 2)
    my_plane = lax.rem(me // 2, planes)
    my_group = (me // (2 * planes)) * 2 + my_core

    def long_of(group, plane):
        return (group // 2) * (2 * planes) + 2 * plane + lax.rem(group, 2)

    peers_a = [long_of(lax.rem(my_group + k, groups), my_plane) for k in range(1, groups)]
    peers_b = [long_of(my_group, lax.rem(my_plane + k, planes)) for k in range(1, planes)]
    barrier = pltpu.get_barrier_semaphore()
    for peer in peers_a + peers_b:
        pl.semaphore_signal(barrier, inc=1, device_id=(peer, column), device_id_type=MESH)
    pl.semaphore_wait(barrier, len(peers_a) + len(peers_b))
    copies = []
    for k in range(1, groups):
        copy = pltpu.make_async_remote_copy(
            src_ref=chunks_ref.at[lax.rem(my_group + k, groups)],
            dst_ref=recv_a.at[k],
            send_sem=send_a.at[k],
            recv_sem=got_a.at[k],
            device_id=(peers_a[k - 1], column),
            device_id_type=MESH,
        )
        copy.start()
        copies.append(copy)
    acc = chunks_ref[my_group]
    for k in range(1, groups):
        copies[k - 1].wait()
        acc = acc + recv_a[k]
    partial[...] = acc
    copies = []
    for k in range(1, planes):
        copy = pltpu.make_async_remote_copy(
            src_ref=partial.at[lax.rem(my_plane + k, planes)],
            dst_ref=recv_b.at[k],
            send_sem=send_b.at[k],
            recv_sem=got_b.at[k],
            device_id=(peers_b[k - 1], column),
            device_id_type=MESH,
        )
        copy.start()
        copies.append(copy)
    total = partial[my_plane]
    for k in range(1, planes):
        copies[k - 1].wait()
        total = total + recv_b[k]
    out_ref[...] = total


PLANES = 4


def reduce_rows(term, wells, window, step, collective_id):
    count = lax.axis_size("long")
    planes = PLANES
    groups = count // planes
    cols = term.shape[1]
    edge = (window - step) // 2
    flat_wells = wells.reshape(1, -1)
    slot = lax.broadcasted_iota(jnp.int32, (count * window, 1), 0)
    group = slot // (planes * window)
    plane = (slot // window) % planes
    owner = (group // 2) * (2 * planes) + 2 * plane + group % 2
    target_row = owner * step - edge + slot % window
    spread = jnp.where(flat_wells // cols == target_row, term.reshape(1, -1), 0.0)
    picks = flat_wells.reshape(-1, 1) % cols == lax.broadcasted_iota(jnp.int32, (1, cols), 1)
    chunks = jnp.dot(spread, picks.astype(jnp.float32), precision=lax.Precision.HIGH)
    chunks = chunks.reshape(groups, planes, window, cols)
    return pl.pallas_call(
        functools.partial(exchange_kernel, planes),
        out_shape=jax.ShapeDtypeStruct((window, cols), jnp.float32),
        in_specs=[pl.BlockSpec(memory_space=pltpu.VMEM)],
        out_specs=pl.BlockSpec(memory_space=pltpu.VMEM),
        scratch_shapes=[
            pltpu.VMEM((planes, window, cols), jnp.float32),
            pltpu.VMEM((groups, planes, window, cols), jnp.float32),
            pltpu.VMEM((planes, window, cols), jnp.float32),
            pltpu.SemaphoreType.DMA((groups,)),
            pltpu.SemaphoreType.DMA((groups,)),
            pltpu.SemaphoreType.DMA((planes,)),
            pltpu.SemaphoreType.DMA((planes,)),
        ],
        compiler_params=pltpu.CompilerParams(collective_id=collective_id, has_side_effects=True),
    )(chunks)


def shards(
    column_seed, head_seed, texture, soil_table, active, conductance, wells, transmissivity, storage
):
    local_rows = column_seed.shape[2]
    local_cols = column_seed.shape[3]
    total_rows = local_rows * lax.axis_size("long")
    total_cols = local_cols * lax.axis_size("aq")
    row_start = lax.axis_index("long") * local_rows
    col_start = lax.axis_index("aq") * local_cols
    heat_1, heat_2, c_sol, d_sol, b_sol, a_last = column_solves(soil_table, texture, column_seed)
    gain = jnp.where(active == 1, conductance, 0.0)

    fields = aq_halo(jnp.stack([head_seed, transmissivity, storage]), HALO)
    fields = jnp.pad(fields, ((0, 0), (HALO, HALO), (0, 0)))
    head_ext, trans_ext, storage_ext = fields[0], fields[1], fields[2]
    ext_rows, ext_cols = head_ext.shape
    row_ids = lax.broadcasted_iota(jnp.int32, (ext_rows, ext_cols), 0) - HALO
    col_ids = col_start - HALO + lax.broadcasted_iota(jnp.int32, (ext_rows, ext_cols), 1)
    valid = (row_ids >= 0) & (row_ids < total_rows) & (col_ids >= 0) & (col_ids < total_cols)
    tp = jnp.pad(trans_ext, 1)
    centre = tp[1:-1, 1:-1]
    east_face = jnp.where(valid & (row_ids + 1 < total_rows), 0.5 * (centre + tp[2:, 1:-1]), 0.0)
    west_face = jnp.where(valid & (row_ids >= 1), 0.5 * (centre + tp[:-2, 1:-1]), 0.0)
    north_face = jnp.where(valid & (col_ids + 1 < total_cols), 0.5 * (centre + tp[1:-1, 2:]), 0.0)
    south_face = jnp.where(valid & (col_ids >= 1), 0.5 * (centre + tp[1:-1, :-2]), 0.0)
    diagonal = storage_ext + east_face + west_face + north_face + south_face
    diagonal = jnp.where(valid, diagonal, 1.0)
    face_set = (east_face, west_face, north_face, south_face)

    window = local_rows + 2 * HALO

    def window_of(a):
        return lax.dynamic_slice_in_dim(a, row_start, window, 0)

    face_win = tuple(window_of(f) for f in face_set)
    diag_win = window_of(diagonal)
    core = slice(HALO, HALO + local_rows), slice(HALO, HALO + local_cols)

    estimate_1 = relax(head_ext, face_set, diagonal)
    recharge_1_win = window_of(estimate_1)[:, HALO:HALO + local_cols]
    recharge_1 = recharge_1_win[HALO:HALO + local_rows]
    r_1 = gain * recharge_1
    term_1 = gain * (a_last + r_1 * b_sol[-1])
    head_1_win = recharge_1_win + reduce_rows(term_1, wells, window, local_rows, 0)

    head_1_ext = aq_halo(head_1_win, HALO)
    estimate_2 = relax(head_1_ext, face_win, diag_win)
    recharge_2 = estimate_2[core]
    r_2 = gain * recharge_2
    term_2 = gain * (c_sol[-1] + r_1 * d_sol[-1] + r_2 * b_sol[-1])
    head_2 = recharge_2 + reduce_rows(term_2, wells, local_rows, local_rows, 1)
    water_2 = c_sol + r_1 * d_sol + r_2 * b_sol
    return (jnp.stack([water_2, heat_2]), recharge_2, head_2)


def solution(mesh):
    return jax.shard_map(
        shards,
        mesh=mesh,
        in_specs=(
            P(None, None, "long", "aq"),
            P(None, "aq"),
            P(None, "long", "aq"),
            P(),
            P("long", "aq"),
            P("long", "aq"),
            P("long", "aq"),
            P(None, "aq"),
            P(None, "aq"),
        ),
        out_specs=(P(None, None, "long", "aq"), P("long", "aq"), P("long", "aq")),
        check_vma=False,
    )
```
